32 devices in a mesh: chan: 4 (over z), tm: 8 (over y, x, core).
Axes of the slice: x: 2, y: 2, z: 4, core: 2. Of those that a mesh axis runs over, the one named last changes fastest.
Arguments:
- voltages: bfloat16 [2, 64, 4, 524288], P(None, 'tm', 'chan'), may hold values from -6 to 6
- antenna_gains: float32 [2, 64, 4], P(None, None, 'chan'), may hold values from -0.75 to 0.75
- chirp_phase: float32 [4, 131072], P('chan'), may hold values from -3.140625 to 3.140625
- offsets: int32 [4], P('chan'), may hold values from 0 to 4095, as said below
- flags: int32 [4, 512], P('chan', 'tm'), may hold values 0 or 1
- sample_phase_bins: int32 [524288], P('tm'), may hold values from 0 to 2047
Outputs:
- dedispersed: bfloat16 [2, 4, 524288], P(None, 'chan', 'tm')
- sk_weight: float32 [4, 512], P('chan', 'tm')
- profile: float32 [4, 2048], P('chan', 'tm')
- band_profile: float32 [2048], P('tm')
The draws below stay inside these ranges and needn't reach their ends.
Inputs may be any that keep to these rules, and one draw needn't show every extreme that they name: `offsets`: some channel has the offset 4096 - 1.
All inputs are finite; a program needn't handle non-finite values. No bound on the sum of `flags` on one device may be relied on, other than what follows from the above.
Results may differ from the reference program's by a relative error of at most 0.0045.
Values may be sent and summed in bfloat16 or wider, within the bound.
A program may use at most 192 MiB of HBM per device.

```python
import jax
import jax.numpy as jnp
from jax import lax

ANTENNA_COUNT = 64
NFFT = 131072
OFFSET_BOUND = 4096
SKW = 1024
BINS = 2048
TS = 65536
CHANNEL_COUNT = 4
TIME_SAMPLES = 524288
NWIN = 512
N_TM = 8


def draw_offsets(key, part):
    values = jax.random.randint(jax.random.fold_in(key, 11), (CHANNEL_COUNT,), 0, OFFSET_BOUND, dtype=jnp.int32)
    chosen = jax.random.randint(jax.random.fold_in(key, 12), (), 0, CHANNEL_COUNT, dtype=jnp.int32)
    marker = jnp.arange(CHANNEL_COUNT, dtype=jnp.int32) == chosen
    return jnp.where(marker, OFFSET_BOUND - 1, values).astype(jnp.int32)


def place_ends(array, key, smallest, top_value):
    extent = array.shape
    spot = [jax.random.randint(jax.random.fold_in(key, axis), (), 0, extent[axis]) for axis in range(len(extent))]
    array = array.at[tuple(spot)].set(smallest)
    longest = extent.index(max(extent))
    spot[longest] = (spot[longest] + 1) % extent[longest]
    return array.at[tuple(spot)].set(top_value)


def with_spikes(drawn, rng, source, target, blocks, factor):
    def block_of(dim):
        return (jnp.arange(drawn.shape[dim]) // (drawn.shape[dim] // blocks)).reshape((-1,) + (1,) * (drawn.ndim - 1 - dim))

    near = jax.random.permutation(rng, blocks)[block_of(target)]
    far = (block_of(target) + blocks // 2) % blocks
    return jnp.where((block_of(source) == near) | (block_of(source) == far), factor * drawn, drawn)


def steps_of(rng, shape, shards, smallest, top_value):
    level, own = 1.0, jax.random.fold_in(rng, 6)
    for axis_at, parts in shards:
        draws = jnp.exp(jax.random.uniform(jax.random.fold_in(own, axis_at), (parts,), jnp.float32, smallest / len(shards), top_value / len(shards)))
        level = level * jnp.repeat(draws, shape[axis_at] // parts).reshape([-1 if axis == axis_at else 1 for axis in range(len(shape))])
    return level


def scatter_about(key, extent, scale, reach, shards=(), held_as=jnp.bfloat16):
    level = steps_of(key, extent, shards, -0.22, 0.18) if shards else 1.0
    values = jax.random.normal(key, extent, jnp.float32) * scale * level
    return jnp.minimum(jnp.maximum(values, -reach), reach).astype(held_as)


def heavy_noise(own_key, extent, spread, bound, pieces, heavy, held_as=jnp.bfloat16):
    entries = spread * jax.random.normal(own_key, extent, jnp.float32)
    if pieces:
        entries = entries * steps_of(own_key, extent, pieces, -0.22, 0.18)
    return jnp.clip(with_spikes(entries, jax.random.fold_in(own_key, 3), *heavy), -bound, bound).astype(held_as)


def setup_inputs(seed: int = 0) -> dict:
    seeds = jax.random.split(jax.random.key(seed), 7)
    voltages = heavy_noise(seeds[0], (2, ANTENNA_COUNT, CHANNEL_COUNT, TIME_SAMPLES), 1.0, 6.0, ((1, 8), (2, 4)), (1, 3, 8, 2.0))
    antenna_gains = scatter_about(seeds[1], (2, ANTENNA_COUNT, CHANNEL_COUNT), ANTENNA_COUNT ** -0.5, 0.75, ((2, 4),), jnp.float32)
    chirp_phase = jnp.clip(jax.random.uniform(seeds[2], (CHANNEL_COUNT, NFFT), jnp.float32, -3.140625, 3.140625), -3.140625, 3.140625)
    offsets = draw_offsets(jax.random.fold_in(seeds[6], 71), 0)
    flags = place_ends((jax.random.randint(seeds[4], (CHANNEL_COUNT, NWIN), 0, 8) < 1).astype(jnp.int32), jax.random.fold_in(seeds[4], 1), 0, 1)
    sample_phase_bins = place_ends(jax.random.randint(seeds[5], (TIME_SAMPLES,), 0, BINS), jax.random.fold_in(seeds[5], 1), 0, BINS - 1).astype(jnp.int32)
    return {"voltages": voltages, "antenna_gains": antenna_gains, "chirp_phase": chirp_phase, "offsets": offsets, "flags": flags, "sample_phase_bins": sample_phase_bins}


SK_WIDTH = 0.05
EPSILON = 1e-6


def reference(voltages, antenna_gains, chirp_phase, offsets, flags, sample_phase_bins):
    def beam_channel(channel):
        samples = lax.dynamic_index_in_dim(voltages, channel, 2, keepdims=False).astype(jnp.float32)
        weights = lax.dynamic_index_in_dim(antenna_gains, channel, 2, keepdims=False)
        weight_real = weights[0][:, None]
        weight_imag = weights[1][:, None]
        out_real = jnp.sum(weight_real * samples[0] - weight_imag * samples[1], axis=0)
        out_imag = jnp.sum(weight_real * samples[1] + weight_imag * samples[0], axis=0)
        return jnp.stack([out_real, out_imag])

    beam_sum = lax.map(beam_channel, jnp.arange(CHANNEL_COUNT, dtype=jnp.int32))

    def dedisperse_channel(items):
        beam_pair, phase_row, start_at = items
        padded = jnp.pad(beam_pair, ((0, 0), (TS, TS)))
        shifted = lax.dynamic_slice_in_dim(padded, start_at.astype(jnp.int32), TIME_SAMPLES + TS, 1)
        blocks = shifted.reshape(2, N_TM + 1, TS)
        segments = jnp.concatenate([blocks[:, :-1], blocks[:, 1:]], axis=2)
        signal = lax.complex(segments[0], segments[1])
        response = lax.complex(jnp.cos(phase_row), jnp.sin(phase_row))
        spectrum = jnp.fft.fft(signal, axis=-1) * response[None, :]
        result = jnp.fft.ifft(spectrum, axis=-1)[:, TS:].reshape(TIME_SAMPLES)
        return jnp.stack([jnp.real(result), jnp.imag(result)])

    output_pair = lax.map(dedisperse_channel, (beam_sum, chirp_phase, offsets))
    output_pair = jnp.moveaxis(output_pair, 1, 0)
    dedispersed = output_pair.astype(jnp.bfloat16)
    power = output_pair[0] * output_pair[0] + output_pair[1] * output_pair[1]
    windows = power.reshape(CHANNEL_COUNT, NWIN, SKW)
    first_sum = jnp.sum(windows, axis=-1)
    second_sum = jnp.sum(windows * windows, axis=-1)
    kurtosis = (SKW + 1.0) / (SKW - 1.0) * (SKW * second_sum / (first_sum * first_sum + EPSILON) - 1.0)
    keep = (1 - flags).astype(jnp.float32)
    sk_weight = keep / (1.0 + ((kurtosis - 1.0) / SK_WIDTH) ** 2)
    weighted = (sk_weight[:, :, None] * windows).reshape(CHANNEL_COUNT, TIME_SAMPLES).astype(jnp.bfloat16)

    def fold_channel(row_values):
        return jax.ops.segment_sum(row_values.astype(jnp.float32), sample_phase_bins, BINS)

    profile = jax.vmap(fold_channel)(weighted) * (BINS / TIME_SAMPLES)
    band_profile = jnp.sum(profile, axis=0)
    return dedispersed, sk_weight, profile, band_profile
```

```python
import functools
import math

import jax
import jax.numpy as jnp
import numpy as np
from jax import lax
from jax.experimental import pallas as pl
from jax.experimental.pallas import tpu as pltpu
from jax.sharding import PartitionSpec as P

NFFT = 131072
OFFSET_BOUND = 4096
SKW = 1024
BINS = 2048


SK_WIDTH = 0.05
EPSILON = 1e-06

COLS = 1 << (NFFT.bit_length() - 1) // 2
ROWS = NFFT // COLS
HALF_ROWS = ROWS // 2
HALO_ROWS = OFFSET_BOUND // COLS
WIN_ROWS = SKW // COLS
WINDOWS = HALF_ROWS // WIN_ROWS
LOW_BINS = 32
HIGH_BINS = BINS // LOW_BINS
BEAM_TILE = 8192
ROW_STEP = 8


def shifted(value, axis, steps):
    count = lax.axis_size(axis)
    first, last = (max(0, -steps), min(count, count - steps))
    return lax.ppermute(value, axis, [(source, source + steps) for source in range(first, last)])


def bf16_split(table):
    high = table.astype(jnp.bfloat16)
    low = (table - high.astype(np.float32)).astype(jnp.bfloat16)
    return np.stack([high, low])


def dft_parts(length):
    index = np.arange(length, dtype=np.int64)
    angle = -2.0 * math.pi / length * (index[:, None] * index[None, :] % length)
    real, imag = (np.cos(angle).astype(np.float32), np.sin(angle).astype(np.float32))
    return np.stack([bf16_split(real), bf16_split(imag)])


def twiddle(row_total, col_total):
    turns = np.arange(row_total, dtype=np.int64)[:, None] * np.arange(col_total, dtype=np.int64) % NFFT
    angle = -2.0 * math.pi / NFFT * turns
    return np.stack([np.cos(angle), np.sin(angle)]).astype(np.float32)


def split(value):
    high = value.astype(jnp.bfloat16)
    return high, (value - high.astype(jnp.float32)).astype(jnp.bfloat16)


def three_pass(left, right, dims):
    def product(a, b):
        return lax.dot_general(a, b, (dims, ((), ())), preferred_element_type=jnp.float32)

    return product(left[0], right[0]) + (product(left[0], right[1]) + product(left[1], right[0]))


def table_times(table, pair, dims, sign):
    real, imag = (split(pair[0]), split(pair[1]))
    rr = three_pass(table[0], real, dims)
    ii = three_pass(table[1], imag, dims)
    ri = three_pass(table[0], imag, dims)
    ir = three_pass(table[1], real, dims)
    if sign > 0:
        return rr - ii, ri + ir
    return rr + ii, ri - ir


def cos_sin(angle):
    half = 0.5 * angle
    square = half * half
    sine = jnp.full_like(square, 1.0 / math.factorial(13))
    for power in (11, 9, 7, 5, 3, 1):
        sine = sine * square + (-1.0) ** (power // 2) / math.factorial(power)
    sine = sine * half
    cosine = jnp.full_like(square, 1.0 / math.factorial(12))
    for power in (10, 8, 6, 4, 2, 0):
        cosine = cosine * square + (-1.0) ** (power // 2) / math.factorial(power)
    return 1.0 - 2.0 * sine * sine, 2.0 * sine * cosine


def beam_kernel(weight_ref, volt_ref, out_ref):
    weights = weight_ref[...]
    total = jnp.dot(weights[0], volt_ref[0, 0], preferred_element_type=jnp.float32)
    total += jnp.dot(weights[1], volt_ref[1, 0], preferred_element_type=jnp.float32)
    out_ref[0, 0] = (total[0:2] + (total[2:4] + total[4:6])).astype(jnp.bfloat16)


def beamform(voltages, weights, shards):
    antennas, channels, samples = voltages.shape[1:]
    block = samples // shards
    tile = min(BEAM_TILE, block)
    steps = block // tile
    real, imag = (weights[0], weights[1])
    on_real = jnp.stack([real, imag])
    on_imag = jnp.stack([-imag, real])
    both = jnp.stack([on_real, on_imag])
    first, rest = split(both)
    second = rest
    third = (both - first.astype(jnp.float32) - second.astype(jnp.float32)).astype(jnp.bfloat16)
    table = jnp.concatenate([first, second, third], axis=1)
    table = jnp.moveaxis(table, 3, 0)
    table = jnp.pad(table, ((0, 0), (0, 0), (0, 2), (0, 0)))
    moved = jnp.transpose(voltages, (0, 2, 1, 3))
    outs = []
    for channel in range(channels):
        outs.append(
            pl.pallas_call(
                beam_kernel,
                out_shape=jax.ShapeDtypeStruct((shards, 1, 2, block), jnp.bfloat16),
                grid=(shards * steps,),
                in_specs=[
                    pl.BlockSpec((2, 8, antennas), lambda i: (0, 0, 0)),
                    pl.BlockSpec(
                        (2, 1, antennas, tile), lambda i, channel=channel: (0, channel, 0, i)
                    ),
                ],
                out_specs=pl.BlockSpec((1, 1, 2, tile), lambda i: (i // steps, 0, 0, i % steps)),
                cost_estimate=pl.CostEstimate(
                    flops=64 * samples * antennas,
                    bytes_accessed=4 * samples * antennas,
                    transcendentals=0,
                ),
                name="beam",
            )(table[channel], moved)
        )
    return outs[0] if channels == 1 else jnp.concatenate(outs, axis=1)


def fold_kernel(
    offset_ref, wide_ref, chirp_ref, keep_ref, bins_ref, outer_ref, inner_ref, twist_ref,
    twist_back_ref, dedispersed_ref, weight_ref, profile_ref, weighted_ref,
):
    offset = offset_ref[0]
    whole, part = (offset // COLS, offset % COLS)
    lane = lax.broadcasted_iota(jnp.int32, (ROWS, COLS), 1)
    turn = lax.rem(COLS - part, COLS)
    base = pl.multiple_of(whole // 8 * 8, 8)
    lift = lax.rem(ROWS + 8 - whole % 8, ROWS + 8)
    signal = []
    for half in range(2):
        loaded = wide_ref[half, pl.ds(base, ROWS + 8), :]
        loaded = pltpu.roll(pltpu.roll(loaded, lift, 0), turn, 1)
        signal.append(jnp.where(lane < COLS - part, loaded[:ROWS], loaded[1 : ROWS + 1]))

    def table(ref, rows=slice(None)):
        return [[ref[0, 0, rows], ref[0, 1, rows]], [ref[1, 0, rows], ref[1, 1, rows]]]

    plain, turned = (((1,), (0,)), ((1,), (1,)))
    real, imag = table_times(table(outer_ref), signal, plain, 1)
    cosine, sine = (twist_ref[0], twist_ref[1])
    real, imag = (real * cosine - imag * sine, real * sine + imag * cosine)
    real, imag = table_times(table(inner_ref), (real, imag), turned, 1)
    cosine, sine = cos_sin(chirp_ref[...])
    real, imag = (real * cosine - imag * sine, real * sine + imag * cosine)
    real, imag = table_times(table(inner_ref), (real, imag), plain, -1)
    cosine, sine = (twist_back_ref[0], twist_back_ref[1])
    real, imag = (real * cosine + imag * sine, imag * cosine - real * sine)
    real, imag = table_times(
        table(outer_ref, slice(HALF_ROWS, ROWS)), (real, imag), turned, -1
    )
    real, imag = (real * (1.0 / NFFT), imag * (1.0 / NFFT))
    dedispersed_ref[0] = real.astype(jnp.bfloat16)
    dedispersed_ref[1] = imag.astype(jnp.bfloat16)
    power = real * real + imag * imag

    def exact_dot(a, b):
        return jnp.dot(a, b, precision=lax.Precision.HIGHEST, preferred_element_type=jnp.float32)

    def owner(shape, axis):
        rows = lax.broadcasted_iota(jnp.int32, shape, axis)
        windows = lax.broadcasted_iota(jnp.int32, shape, 1 - axis)
        return jnp.where(rows // WIN_ROWS == windows, 1.0, 0.0).astype(jnp.float32)

    gather = owner((WINDOWS, HALF_ROWS), 1)
    first_sum = jnp.sum(exact_dot(gather, power), axis=1, keepdims=True)
    second_sum = jnp.sum(exact_dot(gather, power * power), axis=1, keepdims=True)
    kurtosis = (
        (SKW + 1.0) / (SKW - 1.0) * (SKW * second_sum / (first_sum * first_sum + EPSILON) - 1.0)
    )
    scaled = (kurtosis - 1.0) / SK_WIDTH
    sk_weight = keep_ref[...] / (1.0 + scaled * scaled)
    sk_weight = jnp.broadcast_to(sk_weight, (WINDOWS, COLS))
    weight_ref[...] = sk_weight[:, :128]
    spread_weight = exact_dot(owner((HALF_ROWS, WINDOWS), 0), sk_weight)
    weighted_ref[...] = (spread_weight * power).astype(jnp.bfloat16).astype(jnp.float32)

    high_index = lax.broadcasted_iota(jnp.int32, (HIGH_BINS, COLS), 0)
    low_index = lax.broadcasted_iota(jnp.int32, (LOW_BINS, COLS), 0)

    def step(at, total):
        rows = pl.ds(pl.multiple_of(at * ROW_STEP, ROW_STEP), ROW_STEP)
        bins, values = (bins_ref[rows, :], weighted_ref[rows, :])
        high, low = (bins // LOW_BINS, bins % LOW_BINS)
        left, right = ([], [])
        for row in range(ROW_STEP):
            left.append(
                jnp.where(high_index == high[row : row + 1], 1.0, 0.0).astype(jnp.bfloat16)
            )
            right.append(
                jnp.where(low_index == low[row : row + 1], values[row : row + 1], 0.0).astype(
                    jnp.bfloat16
                )
            )
        return total + lax.dot_general(
            jnp.concatenate(left, axis=1),
            jnp.concatenate(right, axis=1),
            (turned, ((), ())),
            preferred_element_type=jnp.float32,
        )

    profile_ref[...] = lax.fori_loop(
        0, HALF_ROWS // ROW_STEP, step, jnp.zeros((HIGH_BINS, LOW_BINS), jnp.float32)
    )


def fold(offset, wide, chirp, keep, bins):
    vmem = pl.BlockSpec(memory_space=pltpu.VMEM)
    tables = (dft_parts(ROWS), dft_parts(COLS), twiddle(ROWS, COLS), twiddle(COLS, ROWS))
    return pl.pallas_call(
        fold_kernel,
        out_shape=(
            jax.ShapeDtypeStruct((2, HALF_ROWS, COLS), jnp.bfloat16),
            jax.ShapeDtypeStruct((WINDOWS, 128), jnp.float32),
            jax.ShapeDtypeStruct((HIGH_BINS, LOW_BINS), jnp.float32),
        ),
        in_specs=[pl.BlockSpec(memory_space=pltpu.SMEM)] + [vmem] * 8,
        out_specs=(vmem,) * 3,
        scratch_shapes=[pltpu.VMEM((HALF_ROWS, COLS), jnp.float32)],
        compiler_params=pltpu.CompilerParams(vmem_limit_bytes=40 << 20),
        cost_estimate=pl.CostEstimate(
            flops=6 * 10**9, bytes_accessed=6 << 20, transcendentals=0
        ),
        name="fold",
    )(offset, wide, chirp, keep, bins, *[jnp.asarray(table) for table in tables])


def on_device(voltages, antenna_gains, chirp_phase, offsets, flags, sample_phase_bins):
    shards = lax.axis_size("tm")
    my_index = lax.axis_index("tm")
    half_length = NFFT // 2
    channels_here = voltages.shape[2]
    antennas_here = voltages.shape[1]
    own_weights = lax.dynamic_slice_in_dim(
        antenna_gains, my_index * antennas_here, antennas_here, 1
    )
    partial_beam = beamform(voltages, own_weights, shards)
    pieces = lax.all_to_all(partial_beam, "tm", 0, 0, tiled=True)
    beam_sum = jnp.sum(pieces.astype(jnp.float32), axis=0)
    beam_sum = beam_sum.reshape(channels_here, 2, HALF_ROWS, COLS)
    earlier = shifted(beam_sum, "tm", 1)
    later = shifted(beam_sum[:, :, :HALO_ROWS], "tm", -1)
    wide = jnp.concatenate([earlier, beam_sum, later], axis=2)
    chirp = chirp_phase.reshape(channels_here, COLS, ROWS)
    keep = (1 - flags).astype(jnp.float32)[:, :, None]
    bins = sample_phase_bins.reshape(HALF_ROWS, COLS)
    results = [
        fold(offsets[at : at + 1], wide[at], chirp[at], keep[at], bins)
        for at in range(channels_here)
    ]
    dedispersed = jnp.stack([item[0].reshape(2, half_length) for item in results], axis=1)
    sk_weight = jnp.stack([item[1][:, 0] for item in results])
    partial_profile = jnp.stack([item[2].reshape(BINS) for item in results])
    blocks = jnp.moveaxis(partial_profile.reshape(channels_here, shards, BINS // shards), 1, 0)
    gathered = lax.all_to_all(blocks, "tm", 0, 0, tiled=True)
    profile = jnp.sum(gathered, axis=0) * (BINS / (half_length * shards))
    band_profile = jnp.sum(lax.all_gather(jnp.sum(profile, axis=0), "chan"), axis=0)
    return (dedispersed, sk_weight, profile, band_profile)


def solution(mesh):
    placed = (
        P(None, "tm", "chan", None),
        P(None, None, "chan"),
        P("chan", None),
        P("chan"),
        P("chan", "tm"),
        P("tm"),
    )
    return jax.shard_map(
        on_device,
        mesh=mesh,
        in_specs=placed,
        out_specs=(P(None, "chan", "tm"), P("chan", "tm"), P("chan", "tm"), P("tm")),
        check_vma=False,
    )
```
